32 devices in a mesh: scenes: 2 (over x), rows: 16 (over z, y, core).
Axes of the slice: x: 2, y: 2, z: 4, core: 2. Of those that a mesh axis runs over, the one named last changes fastest.
Arguments:
- images: float32 [64, 128, 128], P(('scenes', 'rows')), parts along dimension 0, may hold values from -6 to 6
- conv_weight: float32 [3, 3, 128, 128], replicated, may hold values from -0.1875 to 0.1875
- lift_weight: float32 [320, 128], replicated, may hold values from -0.5 to 0.5
- vol_weight: float32 [3, 3, 3, 32, 40], replicated, may hold values from -0.1875 to 0.1875
Outputs:
- filtered: float32 [64, 32, 48, 128], P(('scenes', 'rows')), parts along dimension 0
The draws below stay inside these ranges and needn't reach their ends.
There are 2 independent parts, one for each index of `scenes`. The reference program is written for one: setup_inputs(seed, part) draws one part's arguments, and reference() takes and returns one part's arrays. A program takes and returns all parts, laid end to end along the dimension named above; an argument that names none is the same for every part. Nothing has to cross between parts.
All inputs are finite; a program needn't handle non-finite values.
Results may differ from the reference program's by a relative error of at most 0.0001.
Values sent between devices are 32-bit elements; how exact they have to be, the bound alone decides.
A program may use at most 128 MiB of HBM per device.

```python
import jax
import jax.numpy as jnp
from jax import lax

CIN = 128
FEAT = 320
GROUPS = 40
DISP = 48
OUTC = 32
COLS = 128
HEIGHT = 16


def block_scale(stream_key, dims, pieces, least, largest):
    factor_of = 1.0
    for position, blocks in pieces:
        heights = jax.random.uniform(jax.random.fold_in(jax.random.fold_in(stream_key, 6), position), (blocks,), jnp.float32, least / len(pieces), largest / len(pieces))
        factor_of = factor_of * jnp.repeat(jnp.exp(heights), dims[position] // blocks).reshape((-1,) + (1,) * (len(dims) - 1 - position))
    return factor_of


def centred(rng, shape, spread, most, split=(), dtype=jnp.bfloat16):
    factor_of = block_scale(rng, shape, split, -0.22, 0.18) if split else 1.0
    array = jax.random.normal(rng, shape, jnp.float32) * spread * factor_of
    return jnp.minimum(jnp.maximum(array, -most), most).astype(dtype)


def setup_inputs(seed: int = 0, part: int = 0) -> dict:
    seeds = jax.random.split(jax.random.key(seed), 5)
    own_keys = jax.random.split(jax.random.fold_in(seeds[4], part), 5)
    return {
        "images": centred(own_keys[0], (2 * HEIGHT, CIN, COLS), 1.0, 6.0, ((0, 16),), jnp.float32),
        "conv_weight": centred(seeds[1], (3, 3, CIN, CIN), (9 * CIN) ** -0.5, 0.1875, (), jnp.float32),
        "lift_weight": centred(seeds[2], (FEAT, CIN), CIN ** -0.5, 0.5, (), jnp.float32),
        "vol_weight": centred(seeds[3], (3, 3, 3, OUTC, GROUPS), (27 * GROUPS) ** -0.5, 0.1875, (), jnp.float32),
    }


precise = lax.Precision.HIGHEST


def conv_plane(planes, weight, padding):
    result = lax.conv_general_dilated(planes[None], weight, (1, 1), padding, dimension_numbers=("NHCW", "HWOI", "NHCW"), precision=precise)
    return result[0]


def lift_features(weight, hidden):
    return jnp.einsum("fi,ric->rfc", weight, hidden, precision=precise)


def correlate(anchor, other, groups, disparities):
    row_count, channels, columns = anchor.shape
    padded = jnp.pad(other, ((0, 0), (0, 0), (disparities, 0)))
    layers = []
    for offset in range(disparities):
        shifted = padded[:, :, disparities - offset:disparities - offset + columns]
        product = (anchor * shifted).reshape(row_count, groups, channels // groups, columns)
        layers.append(jnp.mean(product, axis=2))
    return jnp.stack(layers, axis=2)


def conv_volume(volume, weight, padding):
    result = lax.conv_general_dilated(volume[None], weight, (1, 1, 1), padding, dimension_numbers=("NHCDW", "HDWOI", "NHCDW"), precision=precise)
    return result[0]


def reference(images, conv_weight, lift_weight, vol_weight):
    middle = images.shape[0] // 2
    offset_rows = middle // 2
    unrolled = jnp.roll(images, -offset_rows, axis=0)
    left_feat = lift_features(lift_weight, jax.nn.relu(conv_plane(unrolled[:middle], conv_weight, ((1, 1), (1, 1)))))
    right_feat = lift_features(lift_weight, jax.nn.relu(conv_plane(unrolled[middle:], conv_weight, ((1, 1), (1, 1)))))
    left_cost = correlate(left_feat, right_feat, GROUPS, DISP)
    right_cost = jnp.flip(correlate(jnp.flip(right_feat, -1), jnp.flip(left_feat, -1), GROUPS, DISP), -1)
    padding = ((1, 1), (1, 1), (1, 1))
    joined = jnp.concatenate([conv_volume(left_cost, vol_weight, padding), conv_volume(right_cost, vol_weight, padding)], axis=0)
    return jnp.roll(joined, offset_rows, axis=0)
```

```python
import jax
import jax.numpy as jnp
from jax import lax
from jax.experimental import pallas as pl
from jax.experimental.pallas import tpu as pltpu
from jax.sharding import PartitionSpec as P

DISP = 48
CHUNK = 4
STEP = 8
MESH = pl.DeviceIdType.MESH
f32, bf16 = jnp.float32, jnp.bfloat16


def split(x):
    hi = x.astype(bf16)
    return hi, (x - hi.astype(f32)).astype(bf16)


def dot(a, b):
    return jnp.dot(a, b, preferred_element_type=f32)


def dot3(stacked, rows, hi, lo):
    both = dot(stacked, hi)
    return both[:rows] + both[rows:] + dot(stacked[:rows], lo)


def taps(y, size, lane):
    cols = y.shape[1]
    before = jnp.where(lane >= 1, pltpu.roll(y[:size], 1, 1), 0.0)
    after = jnp.where(lane < cols - 1, pltpu.roll(y[2 * size :], cols - 1, 1), 0.0)
    return y[size : 2 * size] + before + after


def turned(x, by, is_right):
    cols = x.shape[-1]
    cut = by % cols
    return x if cut == 0 else pltpu.roll(x, jnp.where(is_right, cols - cut, cut), 1)


def place_of():
    position = lax.axis_index("rows")
    quarter = lax.axis_size("rows") // 4
    starts = (position == quarter) | (position == 3 * quarter)
    ends = (position == quarter - 1) | (position == 3 * quarter - 1)
    is_right = (position < quarter) | (position >= 3 * quarter)
    return starts, ends, is_right


def gather(
    images, cw_far, lw_far, vw_far, feat_a, feat_b, vol_2,
    before, after, there, there_before, there_after, vol_f, conv_2, lift_2,
    here, cw, lw, vw, send, recv, load,
):
    me, size = lax.axis_index("rows"), lax.axis_size("rows")
    up, down, partner = [lax.rem(me + by, size) for by in (1, size - 1, size // 2)]
    starts, ends, is_right = place_of()
    half = size // 2
    rows, cin, cols = images.shape
    halo = rows + 2
    feat = lw.shape[0]
    outc, groups = vw.shape[3:]
    per = feat // groups
    depth = halo * groups
    lane = lax.broadcasted_iota(jnp.int32, (1, cols), 1)

    to_first, to_last = me == half - 1, me == half
    from_first, from_last = me == 0, me == size - 1
    mated = to_first | to_last | from_first | from_last
    mate = jnp.where(to_first, 0, jnp.where(to_last, size - 1, jnp.where(from_first, half - 1, half)))

    fills = [(vw_far, vw), (cw_far, cw), (lw_far, lw), (images, here)]
    fills = [pltpu.make_async_copy(x, y, load.at[n]) for n, (x, y) in enumerate(fills)]
    for one in fills:
        one.start()

    barrier = pltpu.get_barrier_semaphore()

    @pl.when(mated)
    def _():
        pl.semaphore_signal(barrier, inc=1, device_id={"rows": mate}, device_id_type=MESH)

    for to in (up, down, partner):
        pl.semaphore_signal(barrier, inc=1, device_id={"rows": to}, device_id_type=MESH)
    @pl.when(mated)
    def _():
        pl.semaphore_wait(barrier, 4)

    @pl.when(jnp.logical_not(mated))
    def _():
        pl.semaphore_wait(barrier, 3)

    def copy(n, source, target, to, out=None):
        return pltpu.make_async_remote_copy(
            src_ref=source,
            dst_ref=target,
            send_sem=send.at[n if out is None else out],
            recv_sem=recv.at[n],
            device_id={"rows": to},
            device_id_type=MESH,
        )

    last, first = pl.ds(rows - 2, 2), pl.ds(0, 2)
    across = copy(0, images, there, partner)
    near = [copy(1, images.at[last], before, up), copy(2, images.at[first], after, down)]
    relays = [copy(3, there.at[last], there_before, up), copy(4, there.at[first], there_after, down)]
    direct = [
        copy(3, images.at[last], there_before, 0, 5),
        copy(4, images.at[first], there_after, size - 1, 6),
    ]
    across.start()

    @pl.when(to_first)
    def _():
        direct[0].start()

    @pl.when(to_last)
    def _():
        direct[1].start()

    for one in near:
        one.start()

    for one in fills:
        one.wait()

    vol_f[...] = jnp.zeros_like(vol_f)
    for dd in range(3):
        for dc in range(3):
            for r in range(rows):
                for dr in range(3):
                    top = (dc * rows + r) * outc
                    left = dd * depth + (r + dr) * groups
                    vol_f[top : top + outc, left : left + groups] = vw[dr, dd, dc] * (1.0 / per)
    m = 3 * rows * outc
    vol_2[:m], vol_2[m:] = split(vol_f[...])
    wide = jnp.concatenate([cw[dr].reshape(3 * cin, cin) for dr in range(3)], axis=1)
    conv_2[: 3 * cin], conv_2[3 * cin :] = split(wide)
    lift = jnp.concatenate([lw[pl.ds(k, groups, stride=per), :] for k in range(per)], axis=0)
    lift_2[:feat], lift_2[feat:] = split(lift)

    def features(above, middle, below, result, cut):
        parts = []
        for s in range(rows + 4):
            if s < 2:
                x = jnp.where(starts, 0.0, above[s])
            elif s < rows + 2:
                x = middle[s - 2]
            else:
                x = jnp.where(ends, 0.0, below[s - 2 - rows])
            parts.append(split(x))
        for r in range(0, halo, 2):
            pair = (r, min(r + 1, halo - 1))
            hi, lo = [
                jnp.concatenate(
                    [jnp.concatenate([parts[t + k][i] for k in range(3)], axis=0) for t in pair], axis=1
                )
                for i in range(2)
            ]
            y = dot3(conv_2[...], 3 * cin, hi, lo)
            hidden = []
            for n, t in enumerate(pair):
                h = jnp.maximum(taps(y[:, n * cols : (n + 1) * cols], cin, lane), 0.0)
                if cut and t == 0:
                    h = jnp.where(starts, 0.0, h)
                if cut and t == halo - 1:
                    h = jnp.where(ends, 0.0, h)
                hidden.append(h)
            f = dot3(lift_2[...], feat, *split(jnp.concatenate(hidden, axis=1)))
            for n, t in enumerate(pair):
                for k in range(per):
                    part = f[k * groups : (k + 1) * groups, n * cols : (n + 1) * cols]
                    result[k, t * groups : (t + 1) * groups, :] = part

    across.wait_recv()

    @pl.when(jnp.logical_not(from_last))
    def _():
        relays[0].start()

    @pl.when(jnp.logical_not(from_first))
    def _():
        relays[1].start()

    for one in near:
        one.wait_recv()
    features(before, here, after, feat_a.at[0], True)
    for b in range(1, STEP):
        for k in range(per):
            feat_a[b, k] = turned(feat_a[0, k], -b, is_right)
    for one in relays:
        one.wait_recv()
    features(there_before, there, there_after, feat_b, False)
    for one in (across, *near):
        one.wait_send()

    @pl.when(jnp.logical_not(from_last))
    def _():
        relays[0].wait_send()

    @pl.when(jnp.logical_not(from_first))
    def _():
        relays[1].wait_send()

    @pl.when(to_first)
    def _():
        direct[0].wait_send()

    @pl.when(to_last)
    def _():
        direct[1].wait_send()


def compute(feat_a, first_b, vol_2, out, feat_b, cost_hi, cost_lo):
    _, _, is_right = place_of()
    per, depth, cols = first_b.shape
    m, padded = vol_2.shape
    m = m // 2
    lane = lax.broadcasted_iota(jnp.int32, (1, cols), 1)

    for buf in (cost_hi, cost_lo):
        buf[:depth] = jnp.zeros((depth, cols), bf16)
        tail = buf.shape[0] - (DISP + 1) * depth
        buf[(DISP + 1) * depth :] = jnp.zeros((tail, cols), bf16)
    reach = jnp.where(is_right, cols - 1 - lane, lane)

    def correlate(disparities):
        for base in range(0, depth, 16):
            at = slice(base, base + 16)
            for d in disparities:
                step, b = divmod(d, STEP)
                total = None
                for k in range(per):
                    if b == 0 and step > 0:
                        feat_b[step, k, at, :] = turned(first_b[k, at, :], STEP * step, is_right)
                    right = feat_b[step, k, at, :] if step else first_b[k, at, :]
                    term = feat_a[b, k, at, :] * right
                    total = term if total is None else total + term
                hi, lo = split(jnp.where(reach >= d, turned(total, b, is_right), 0.0))
                place = (d + 1) * depth + base
                cost_hi[place : place + 16, :] = hi
                cost_lo[place : place + 16, :] = lo

    def filtered(d):
        first, second = d * depth, (d + 1) * depth
        hi, lo = [
            jnp.concatenate([buf[first : first + padded, :], buf[second : second + padded, :]], axis=1)
            for buf in (cost_hi, cost_lo)
        ]
        y = dot3(vol_2[...], m, hi, lo)
        for h in range(2):
            z = taps(y[:, h * cols : (h + 1) * cols], m // 3, lane)
            out[pl.ds(d + h, m // 3, stride=DISP), :] = z

    correlate(range(CHUNK + 2))
    for d in range(0, DISP, CHUNK):
        correlate(range(d + CHUNK + 2, min(d + 2 * CHUNK + 2, DISP)))
        for e in range(d, d + CHUNK, 2):
            filtered(e)


def on_device(images, conv_weight, lift_weight, vol_weight):
    rows, cin, cols = images.shape
    outc, groups = vol_weight.shape[3:]
    feat = lift_weight.shape[0]
    per = feat // groups
    depth = (rows + 2) * groups
    padded = -(-3 * depth // 256) * 256
    m = 3 * rows * outc
    length = DISP * depth + padded
    vmem = pl.BlockSpec(memory_space=pltpu.VMEM)
    edge = pltpu.VMEM((2, cin, cols), f32)
    first_a, first_b, vol_2 = pl.pallas_call(
        gather,
        out_shape=[
            jax.ShapeDtypeStruct((STEP, per, depth, cols), f32),
            jax.ShapeDtypeStruct((per, depth, cols), f32),
            jax.ShapeDtypeStruct((2 * m, padded), bf16),
        ],
        in_specs=[pl.BlockSpec(memory_space=pltpu.HBM)] * 4,
        out_specs=[vmem] * 3,
        scratch_shapes=[
            edge,
            edge,
            pltpu.VMEM((rows, cin, cols), f32),
            edge,
            edge,
            pltpu.VMEM((m, padded), f32),
            pltpu.VMEM((6 * cin, 3 * cin), bf16),
            pltpu.VMEM((2 * feat, cin), bf16),
            pltpu.VMEM(images.shape, f32),
            pltpu.VMEM(conv_weight.shape, f32),
            pltpu.VMEM(lift_weight.shape, f32),
            pltpu.VMEM(vol_weight.shape, f32),
            pltpu.SemaphoreType.DMA((7,)),
            pltpu.SemaphoreType.DMA((5,)),
            pltpu.SemaphoreType.DMA((4,)),
        ],
        compiler_params=pltpu.CompilerParams(
            vmem_limit_bytes=32 << 20, collective_id=0, has_side_effects=True
        ),
    )(*[pltpu.with_memory_space_constraint(x, pltpu.HBM) for x in (images, conv_weight, lift_weight, vol_weight)])
    flat = pl.pallas_call(
        compute,
        out_shape=jax.ShapeDtypeStruct((rows * outc * DISP, cols), f32),
        in_specs=[vmem] * 3,
        out_specs=vmem,
        scratch_shapes=[
            pltpu.VMEM((-(-DISP // STEP), per, depth, cols), f32),
            pltpu.VMEM((length, cols), bf16),
            pltpu.VMEM((length, cols), bf16),
        ],
        compiler_params=pltpu.CompilerParams(vmem_limit_bytes=32 << 20),
    )(first_a, first_b, vol_2)
    return flat.reshape(rows, outc, DISP, cols)


def solution(mesh):
    placed = (P(("scenes", "rows"), None, None), P(), P(), P())
    return jax.shard_map(
        on_device,
        mesh=mesh,
        in_specs=placed,
        out_specs=P(("scenes", "rows"), None, None, None),
        check_vma=False,
    )
```

```python
import jax
import jax.numpy as jnp
from jax import lax
from jax.experimental import pallas as pl
from jax.experimental.pallas import tpu as pltpu
from jax.sharding import PartitionSpec as P

DISP = 48
CHUNK = 4
STEP = 8
CHUNKS = 4
MESH = pl.DeviceIdType.MESH
f32, bf16 = jnp.float32, jnp.bfloat16


def split(x):
    hi = x.astype(bf16)
    return hi, (x - hi.astype(f32)).astype(bf16)


def dot(a, b):
    return jnp.dot(a, b, preferred_element_type=f32)


def dot3(stacked, rows, hi, lo):
    both = dot(stacked, hi)
    return both[:rows] + both[rows:] + dot(stacked[:rows], lo)


def taps(y, size, lane):
    cols = y.shape[1]
    before = jnp.where(lane >= 1, pltpu.roll(y[:size], 1, 1), 0.0)
    after = jnp.where(lane < cols - 1, pltpu.roll(y[2 * size :], cols - 1, 1), 0.0)
    return y[size : 2 * size] + before + after


def turned(x, by, is_right):
    cols = x.shape[-1]
    cut = by % cols
    return x if cut == 0 else pltpu.roll(x, jnp.where(is_right, cols - cut, cut), 1)


def place_of():
    position = lax.axis_index("rows")
    quarter = lax.axis_size("rows") // 4
    starts = (position == quarter) | (position == 3 * quarter)
    ends = (position == quarter - 1) | (position == 3 * quarter - 1)
    is_right = (position < quarter) | (position >= 3 * quarter)
    return starts, ends, is_right


def stacked(x):
    hi, lo = split(x)
    return jnp.concatenate([hi, lo, hi], axis=0)


def weights(x):
    hi, lo = split(x)
    return jnp.concatenate([hi, hi, lo], axis=1)


def gather(
    images, cw_far, lw_far, vw_far, feats, vol_2,
    x, vol_f, conv_w, lift_w, cw, lw, vw, send, recv, load, ready,
):
    me, size = lax.axis_index("rows"), lax.axis_size("rows")
    starts, ends, is_right = place_of()
    half = size // 2
    rows, cin, cols = images.shape
    halo = rows + 2
    feat = lw.shape[0]
    outc, groups = vw.shape[3:]
    per = feat // groups
    depth = halo * groups
    lane = lax.broadcasted_iota(jnp.int32, (1, cols), 1)

    partner = lax.rem(me + half, size)
    late_up = (me == half - 1) | (me == size - 1)
    late_down = (me == 0) | (me == half)
    mated = late_up | late_down
    mate = jnp.where(me >= half, size + half - 1 - me, half - 1 - me)
    up = jnp.where(late_up, mate, lax.rem(me + 1, size))
    down = jnp.where(late_down, mate, lax.rem(me + size - 1, size))
    to_up, to_down = jnp.logical_not(ends), jnp.logical_not(starts)
    view_up = jnp.where(late_up, 1, 0)
    view_down = jnp.where(late_down, 1, 0)

    fills = [(cw_far, cw), (lw_far, lw), (vw_far, vw), (images, x.at[0, pl.ds(2, rows)])]
    fills = [pltpu.make_async_copy(a, b, load.at[n]) for n, (a, b) in enumerate(fills)]
    for one in fills:
        one.start()

    barrier = pltpu.get_barrier_semaphore()
    links = [(True, partner, 0), (to_up, up, 1), (to_down, down, 2)]

    def greet(other):
        pl.semaphore_signal(barrier, inc=1, device_id={"rows": other}, device_id_type=MESH)

    def confirm(other, n):
        pl.semaphore_signal(ready.at[n], inc=1, device_id={"rows": other}, device_id_type=MESH)

    def confirmed(n):
        pl.semaphore_wait(ready.at[n], 1)

    for there, other, _ in links:
        pl.when(there & (other > me))(lambda: greet(other))
    lower = sum(jnp.where(there & (other < me), 1, 0) for there, other, _ in links)
    pl.when(lower > 0)(lambda: pl.semaphore_wait(barrier, lower))
    for there, other, n in links:
        pl.when(there & (other < me))(lambda: confirm(other, (0, 2, 1)[n]))

    def copy(n, source, target, to):
        return pltpu.make_async_remote_copy(
            src_ref=source,
            dst_ref=target,
            send_sem=send.at[n],
            recv_sem=recv.at[n],
            device_id={"rows": to},
            device_id_type=MESH,
        )

    piece = cin // (CHUNKS // rows)
    places = [(r, pl.ds(a, piece)) for r in range(rows) for a in range(0, cin, piece)]
    above, here, below = pl.ds(0, 2), pl.ds(2, 2), pl.ds(rows + 2, 2)
    across = [copy(n, images.at[r, c], x.at[1, 2 + r, c], partner) for n, (r, c) in enumerate(places)]
    near_up = copy(CHUNKS, images.at[pl.ds(rows - 2, 2)], x.at[view_up, above], up)
    near_down = copy(CHUNKS + 1, images.at[pl.ds(0, 2)], x.at[view_down, below], down)
    relay_up = [
        copy(CHUNKS + 2 + n, x.at[1, 2 + r, c], x.at[1 - view_up, r, c], up)
        for n, (r, c) in enumerate(places)
    ]
    relay_down = [
        copy(2 * CHUNKS + 2 + n, x.at[1, 2 + r, c], x.at[1 - view_down, rows + 2 + r, c], down)
        for n, (r, c) in enumerate(places)
    ]
    held = (me >= size - size // 4) & jnp.logical_not(mated)

    def cross():
        for one in across:
            one.start()

    pl.when((partner < me) & jnp.logical_not(held))(cross)

    @pl.when(to_up)
    def _():
        pl.when(up > me)(lambda: confirmed(1))
        near_up.start()

    @pl.when(to_down)
    def _():
        pl.when(down > me)(lambda: confirmed(2))
        near_down.start()

    @pl.when(partner > me)
    def _():
        confirmed(0)
        cross()

    for one in fills:
        one.wait()

    conv_w[...] = weights(jnp.concatenate([cw[dr].reshape(3 * cin, cin) for dr in range(3)], axis=1))
    lift = jnp.concatenate([lw[pl.ds(k, groups, stride=per), :] for k in range(per)], axis=0)
    lift_w[...] = weights(lift)

    def features(v, h):
        parts = []
        for i in range(4):
            outside = (h == 0) & starts if i < 2 else (h == 1) & ends
            parts.append(split(jnp.where(outside, 0.0, x[v, 2 * h + i])))
        hi, lo = [
            jnp.concatenate(
                [jnp.concatenate([parts[t + k][i] for k in range(3)], axis=0) for t in range(2)], axis=1
            )
            for i in range(2)
        ]
        y = dot(conv_w[...], jnp.concatenate([hi, lo, hi], axis=0))
        hidden = []
        for n in range(2):
            z = jnp.maximum(taps(y[:, n * cols : (n + 1) * cols], cin, lane), 0.0)
            outside = (h == 0) & starts if n == 0 else (h == 1) & ends
            hidden.append(jnp.where(outside, 0.0, z))
        f = dot(lift_w[...], stacked(jnp.concatenate(hidden, axis=1)))
        top = pl.multiple_of(h * 2 * groups, 8)
        for n in range(2):
            for k in range(per):
                part = f[k * groups : (k + 1) * groups, n * cols : (n + 1) * cols]
                feats[1 - v, k, pl.ds(top + n * groups, groups), :] = part

    def spread(h):
        top = pl.multiple_of(h * 2 * groups, 8)
        for k in range(per):
            part = feats[1, k, pl.ds(top, 2 * groups), :]
            for b in range(1, STEP):
                feats[1 + b, k, pl.ds(top, 2 * groups), :] = turned(part, -b, is_right)

    vol_f[...] = jnp.zeros_like(vol_f)
    for dd in range(3):
        for dc in range(3):
            for r in range(rows):
                for dr in range(3):
                    top = (dc * rows + r) * outc
                    left = dd * depth + (r + dr) * groups
                    vol_f[top : top + outc, left : left + groups] = vw[dr, dd, dc] * (1.0 / per)
    m = 3 * rows * outc
    vol_2[:m], vol_2[m:] = split(vol_f[...])

    pl.when(held)(cross)
    pl.when(to_down)(near_up.wait_recv)
    pl.when(to_up)(near_down.wait_recv)

    def relay():
        for n in range(CHUNKS):
            across[n].wait_recv()
            pl.when(to_up)(relay_up[n].start)
            pl.when(to_down)(relay_down[n].start)

    def arrived(copies):
        for one in copies:
            one.wait_recv()

    first = 1 - lax.rem(me, 2)

    def own(j, carry):
        h = jnp.where(j == 0, first, 1 - first)
        features(0, h)
        spread(h)
        return carry

    lax.fori_loop(0, jnp.where(mated, 1, 2), own, 0)

    for n in range(CHUNKS):
        across[n].wait_recv()
        pl.when(to_up)(relay_up[n].start)
        pl.when(to_down)(relay_down[n].start)

    def arrived(copies):
        for one in copies:
            one.wait_recv()

    def rest(j, carry):
        h = jnp.where(j == 0, first, 1 - first)
        v = jnp.where(j == 2, 0, 1)
        due = (j == 0) | ((j == 1) & jnp.logical_not(mated)) | (j == 2)
        pl.when(due & to_down & (h == 0))(lambda: arrived(relay_up))
        pl.when(due & to_up & (h == 1))(lambda: arrived(relay_down))
        features(v, h)
        pl.when(j == 2)(lambda: spread(h))
        return carry

    lax.fori_loop(0, jnp.where(mated, 3, 2), rest, 0)

    for one in across:
        one.wait_send()

    pl.when(to_up)(near_up.wait_send)
    pl.when(to_down)(near_down.wait_send)

    @pl.when(to_up)
    def _():
        for one in relay_up:
            one.wait_send()

    @pl.when(to_down)
    def _():
        for one in relay_down:
            one.wait_send()


def compute(feats, vol_2, out, cost_hi, cost_lo, result, done):
    _, _, is_right = place_of()
    _, per, depth, cols = feats.shape
    m, padded = vol_2.shape
    m = m // 2
    lane = lax.broadcasted_iota(jnp.int32, (1, cols), 1)

    for buf in (cost_hi, cost_lo):
        buf[:depth] = jnp.zeros((depth, cols), bf16)
        tail = buf.shape[0] - (DISP + 1) * depth
        buf[(DISP + 1) * depth :] = jnp.zeros((tail, cols), bf16)
    reach = jnp.where(is_right, cols - 1 - lane, lane)

    def correlate(step):
        for base in range(0, depth, 16):
            at = slice(base, base + 16)
            right = [turned(feats[0, k, at, :], STEP * step, is_right) for k in range(per)]
            for b in range(STEP):
                d = STEP * step + b
                total = None
                for k in range(per):
                    term = feats[1 + b, k, at, :] * right[k]
                    total = term if total is None else total + term
                hi, lo = split(jnp.where(reach >= d, turned(total, b, is_right), 0.0))
                place = (d + 1) * depth + base
                cost_hi[place : place + 16, :] = hi
                cost_lo[place : place + 16, :] = lo

    def filtered(d):
        first, second = d * depth, (d + 1) * depth
        hi, lo = [
            jnp.concatenate([buf[first : first + padded, :], buf[second : second + padded, :]], axis=1)
            for buf in (cost_hi, cost_lo)
        ]
        y = dot3(vol_2[...], m, hi, lo)
        for h in range(2):
            flat = result.reshape(m // 3 * DISP, cols)
            flat[pl.ds(d + h, m // 3, stride=DISP), :] = taps(y[:, h * cols : (h + 1) * cols], m // 3, lane)

    def sent(d):
        part = pl.ds(d, STEP)
        return pltpu.make_async_copy(result.at[:, part, :], out.at[:, part, :], done.at[d // STEP])

    correlate(0)
    for step in range(DISP // STEP):
        if step + 1 < DISP // STEP:
            correlate(step + 1)
        last = STEP * step + STEP if step + 1 == DISP // STEP else STEP * step + STEP - 2
        for d in range(max(STEP * step - 2, 0), last, 2):
            filtered(d)
            if d % STEP == STEP - 2:
                sent(d + 2 - STEP).start()
    for d in range(0, DISP, STEP):
        sent(d).wait()


def on_device(images, conv_weight, lift_weight, vol_weight):
    rows, cin, cols = images.shape
    outc, groups = vol_weight.shape[3:]
    feat = lift_weight.shape[0]
    per = feat // groups
    depth = (rows + 2) * groups
    padded = -(-3 * depth // 256) * 256
    m = 3 * rows * outc
    length = DISP * depth + padded
    vmem = pl.BlockSpec(memory_space=pltpu.VMEM)
    feats, vol_2 = pl.pallas_call(
        gather,
        out_shape=[
            jax.ShapeDtypeStruct((1 + STEP, per, depth, cols), f32),
            jax.ShapeDtypeStruct((2 * m, padded), bf16),
        ],
        in_specs=[pl.BlockSpec(memory_space=pltpu.HBM)] * 4,
        out_specs=[vmem] * 2,
        scratch_shapes=[
            pltpu.VMEM((2, rows + 4, cin, cols), f32),
            pltpu.VMEM((m, padded), f32),
            pltpu.VMEM((3 * cin, 9 * cin), bf16),
            pltpu.VMEM((feat, 3 * cin), bf16),
            pltpu.VMEM(conv_weight.shape, f32),
            pltpu.VMEM(lift_weight.shape, f32),
            pltpu.VMEM(vol_weight.shape, f32),
            pltpu.SemaphoreType.DMA((3 * CHUNKS + 2,)),
            pltpu.SemaphoreType.DMA((3 * CHUNKS + 2,)),
            pltpu.SemaphoreType.DMA((4,)),
            pltpu.SemaphoreType.REGULAR((3,)),
        ],
        compiler_params=pltpu.CompilerParams(
            vmem_limit_bytes=32 << 20, collective_id=0, has_side_effects=True
        ),
    )(*[pltpu.with_memory_space_constraint(a, pltpu.HBM) for a in (images, conv_weight, lift_weight, vol_weight)])
    flat = pl.pallas_call(
        compute,
        out_shape=jax.ShapeDtypeStruct((rows * outc, DISP, cols), f32),
        in_specs=[vmem] * 2,
        out_specs=pl.BlockSpec(memory_space=pltpu.HBM),
        scratch_shapes=[
            pltpu.VMEM((length, cols), bf16),
            pltpu.VMEM((length, cols), bf16),
            pltpu.VMEM((rows * outc, DISP, cols), f32),
            pltpu.SemaphoreType.DMA((DISP // STEP,)),
        ],
        compiler_params=pltpu.CompilerParams(
            vmem_limit_bytes=32 << 20
        ),
    )(feats, vol_2)
    return flat.reshape(rows, outc, DISP, cols)


def solution(mesh):
    placed = (P(("scenes", "rows"), None, None), P(), P(), P())
    return jax.shard_map(
        on_device,
        mesh=mesh,
        in_specs=placed,
        out_specs=P(("scenes", "rows"), None, None, None),
        check_vma=False,
    )
```

```python
import jax
import jax.numpy as jnp
from jax import lax
from jax.experimental import pallas as pl
from jax.experimental.pallas import tpu as pltpu
from jax.sharding import PartitionSpec as P

DISP = 48
CHUNK = 4
STEP = 8
CHUNKS = 4
MESH = pl.DeviceIdType.MESH
f32, bf16 = jnp.float32, jnp.bfloat16


def split(x):
    hi = x.astype(bf16)
    return hi, (x - hi.astype(f32)).astype(bf16)


def dot(a, b):
    return jnp.dot(a, b, preferred_element_type=f32)


def dot3(stacked, rows, hi, lo):
    both = dot(stacked, hi)
    return both[:rows] + both[rows:] + dot(stacked[:rows], lo)


def taps(y, size, lane):
    cols = y.shape[1]
    before = jnp.where(lane >= 1, pltpu.roll(y[:size], 1, 1), 0.0)
    after = jnp.where(lane < cols - 1, pltpu.roll(y[2 * size :], cols - 1, 1), 0.0)
    return y[size : 2 * size] + before + after


def turned(x, by, is_right):
    cols = x.shape[-1]
    cut = by % cols
    return x if cut == 0 else pltpu.roll(x, jnp.where(is_right, cols - cut, cut), 1)


def place_of():
    position = lax.axis_index("rows")
    quarter = lax.axis_size("rows") // 4
    starts = (position == quarter) | (position == 3 * quarter)
    ends = (position == quarter - 1) | (position == 3 * quarter - 1)
    is_right = (position < quarter) | (position >= 3 * quarter)
    return starts, ends, is_right


def stacked(x):
    hi, lo = split(x)
    return jnp.concatenate([hi, lo, hi], axis=0)


def weights(x):
    hi, lo = split(x)
    return jnp.concatenate([hi, hi, lo], axis=1)


def gather(
    images, cw_far, lw_far, vw_far, feats, vol_2,
    x, vol_f, conv_w, lift_w, cw, lw, vw, send, recv, load, ready,
):
    me, size = lax.axis_index("rows"), lax.axis_size("rows")
    starts, ends, is_right = place_of()
    half = size // 2
    rows, cin, cols = images.shape
    halo = rows + 2
    feat = lw.shape[0]
    outc, groups = vw.shape[3:]
    per = feat // groups
    depth = halo * groups
    lane = lax.broadcasted_iota(jnp.int32, (1, cols), 1)

    partner = lax.rem(me + half, size)
    late_up = (me == half - 1) | (me == size - 1)
    late_down = (me == 0) | (me == half)
    mated = late_up | late_down
    mate = jnp.where(me >= half, size + half - 1 - me, half - 1 - me)
    up = jnp.where(late_up, mate, lax.rem(me + 1, size))
    down = jnp.where(late_down, mate, lax.rem(me + size - 1, size))
    to_up, to_down = jnp.logical_not(ends), jnp.logical_not(starts)
    view_up = jnp.where(late_up, 1, 0)
    view_down = jnp.where(late_down, 1, 0)

    fills = [(cw_far, cw), (lw_far, lw), (vw_far, vw), (images, x.at[0, pl.ds(2, rows)])]
    fills = [pltpu.make_async_copy(a, b, load.at[n]) for n, (a, b) in enumerate(fills)]
    for one in fills:
        one.start()

    barrier = pltpu.get_barrier_semaphore()
    links = [(True, partner, 0), (to_up, up, 1), (to_down, down, 2)]

    def greet(other):
        pl.semaphore_signal(barrier, inc=1, device_id={"rows": other}, device_id_type=MESH)

    def confirm(other, n):
        pl.semaphore_signal(ready.at[n], inc=1, device_id={"rows": other}, device_id_type=MESH)

    def confirmed(n):
        pl.semaphore_wait(ready.at[n], 1)

    for there, other, _ in links:
        pl.when(there & (other > me))(lambda: greet(other))
    lower = sum(jnp.where(there & (other < me), 1, 0) for there, other, _ in links)
    pl.when(lower > 0)(lambda: pl.semaphore_wait(barrier, lower))
    for there, other, n in links:
        pl.when(there & (other < me))(lambda: confirm(other, (0, 2, 1)[n]))

    def copy(n, source, target, to):
        return pltpu.make_async_remote_copy(
            src_ref=source,
            dst_ref=target,
            send_sem=send.at[n],
            recv_sem=recv.at[n],
            device_id={"rows": to},
            device_id_type=MESH,
        )

    piece = cin // (CHUNKS // rows)
    places = [(r, pl.ds(a, piece)) for r in range(rows) for a in range(0, cin, piece)]
    above, here, below = pl.ds(0, 2), pl.ds(2, 2), pl.ds(rows + 2, 2)
    across = [copy(n, images.at[r, c], x.at[1, 2 + r, c], partner) for n, (r, c) in enumerate(places)]
    near_up = copy(CHUNKS, images.at[pl.ds(rows - 2, 2)], x.at[view_up, above], up)
    near_down = copy(CHUNKS + 1, images.at[pl.ds(0, 2)], x.at[view_down, below], down)
    relay_up = [
        copy(CHUNKS + 2 + n, x.at[1, 2 + r, c], x.at[1 - view_up, r, c], up)
        for n, (r, c) in enumerate(places)
    ]
    relay_down = [
        copy(2 * CHUNKS + 2 + n, x.at[1, 2 + r, c], x.at[1 - view_down, rows + 2 + r, c], down)
        for n, (r, c) in enumerate(places)
    ]
    held = (me >= size - size // 4) & jnp.logical_not(mated)

    def cross():
        for one in across:
            one.start()

    pl.when((partner < me) & jnp.logical_not(held))(cross)

    @pl.when(to_up)
    def _():
        pl.when(up > me)(lambda: confirmed(1))
        near_up.start()

    @pl.when(to_down)
    def _():
        pl.when(down > me)(lambda: confirmed(2))
        near_down.start()

    @pl.when(partner > me)
    def _():
        confirmed(0)
        cross()

    for one in fills:
        one.wait()

    conv_w[...] = weights(jnp.concatenate([cw[dr].reshape(3 * cin, cin) for dr in range(3)], axis=1))
    lift = jnp.concatenate([lw[pl.ds(k, groups, stride=per), :] for k in range(per)], axis=0)
    lift_w[...] = weights(lift)

    def features(v, h):
        parts = []
        for i in range(4):
            outside = (h == 0) & starts if i < 2 else (h == 1) & ends
            parts.append(split(jnp.where(outside, 0.0, x[v, 2 * h + i])))
        hi, lo = [
            jnp.concatenate(
                [jnp.concatenate([parts[t + k][i] for k in range(3)], axis=0) for t in range(2)], axis=1
            )
            for i in range(2)
        ]
        y = dot(conv_w[...], jnp.concatenate([hi, lo, hi], axis=0))
        hidden = []
        for n in range(2):
            z = jnp.maximum(taps(y[:, n * cols : (n + 1) * cols], cin, lane), 0.0)
            outside = (h == 0) & starts if n == 0 else (h == 1) & ends
            hidden.append(jnp.where(outside, 0.0, z))
        f = dot(lift_w[...], stacked(jnp.concatenate(hidden, axis=1)))
        top = pl.multiple_of(h * 2 * groups, 8)
        for n in range(2):
            for k in range(per):
                part = f[k * groups : (k + 1) * groups, n * cols : (n + 1) * cols]
                feats[1 - v, k, pl.ds(top + n * groups, groups), :] = part

    def spread(h):
        top = pl.multiple_of(h * 2 * groups, 8)
        for k in range(per):
            part = feats[1, k, pl.ds(top, 2 * groups), :]
            for b in range(1, STEP):
                feats[1 + b, k, pl.ds(top, 2 * groups), :] = turned(part, -b, is_right)

    vol_f[...] = jnp.zeros_like(vol_f)
    for dd in range(3):
        for dc in range(3):
            for r in range(rows):
                for dr in range(3):
                    top = (dc * rows + r) * outc
                    left = dd * depth + (r + dr) * groups
                    vol_f[top : top + outc, left : left + groups] = vw[dr, dd, dc] * (1.0 / per)
    m = 3 * rows * outc
    vol_2[:m], vol_2[m:] = split(vol_f[...])

    pl.when(held)(cross)
    odd = lax.rem(me, 2) == 1
    first = jnp.where(odd, 0, 1)

    def arrived(copies):
        for one in copies:
            one.wait_recv()

    pl.when(to_down & odd)(near_up.wait_recv)
    pl.when(to_up & jnp.logical_not(odd))(near_down.wait_recv)
    features(0, first)
    spread(first)

    for n in range(CHUNKS):
        across[n].wait_recv()
        pl.when(to_up)(relay_up[n].start)
        pl.when(to_down)(relay_down[n].start)

    pl.when(to_down & jnp.logical_not(odd))(near_up.wait_recv)
    pl.when(to_up & odd)(near_down.wait_recv)

    def rest(j, carry):
        v = jnp.where(mated, jnp.where(j == 2, 0, 1), jnp.where(j == 0, 0, 1))
        h = jnp.where(j == jnp.where(mated, 0, 1), first, 1 - first)
        due = j != jnp.where(mated, 1, 0)
        pl.when(due & to_down & (h == 0))(lambda: arrived(relay_up))
        pl.when(due & to_up & (h == 1))(lambda: arrived(relay_down))
        features(v, h)
        pl.when(v == 0)(lambda: spread(h))
        return carry

    lax.fori_loop(0, 3, rest, 0)

    for one in across:
        one.wait_send()

    pl.when(to_up)(near_up.wait_send)
    pl.when(to_down)(near_down.wait_send)

    @pl.when(to_up)
    def _():
        for one in relay_up:
            one.wait_send()

    @pl.when(to_down)
    def _():
        for one in relay_down:
            one.wait_send()


def compute(feats, vol_2, out, cost_hi, cost_lo, result, done):
    _, _, is_right = place_of()
    _, per, depth, cols = feats.shape
    m, padded = vol_2.shape
    m = m // 2
    lane = lax.broadcasted_iota(jnp.int32, (1, cols), 1)

    for buf in (cost_hi, cost_lo):
        buf[:depth] = jnp.zeros((depth, cols), bf16)
        tail = buf.shape[0] - (DISP + 1) * depth
        buf[(DISP + 1) * depth :] = jnp.zeros((tail, cols), bf16)
    reach = jnp.where(is_right, cols - 1 - lane, lane)

    def correlate(step):
        for base in range(0, depth, 16):
            at = slice(base, base + 16)
            right = [turned(feats[0, k, at, :], STEP * step, is_right) for k in range(per)]
            for b in range(STEP):
                d = STEP * step + b
                total = None
                for k in range(per):
                    term = feats[1 + b, k, at, :] * right[k]
                    total = term if total is None else total + term
                hi, lo = split(jnp.where(reach >= d, turned(total, b, is_right), 0.0))
                place = (d + 1) * depth + base
                cost_hi[place : place + 16, :] = hi
                cost_lo[place : place + 16, :] = lo

    def filtered(d):
        first, second = d * depth, (d + 1) * depth
        hi, lo = [
            jnp.concatenate([buf[first : first + padded, :], buf[second : second + padded, :]], axis=1)
            for buf in (cost_hi, cost_lo)
        ]
        y = dot3(vol_2[...], m, hi, lo)
        for h in range(2):
            flat = result.reshape(m // 3 * DISP, cols)
            flat[pl.ds(d + h, m // 3, stride=DISP), :] = taps(y[:, h * cols : (h + 1) * cols], m // 3, lane)

    def sent(d):
        part = pl.ds(d, STEP)
        return pltpu.make_async_copy(result.at[:, part, :], out.at[:, part, :], done.at[d // STEP])

    correlate(0)
    for step in range(DISP // STEP):
        if step + 1 < DISP // STEP:
            correlate(step + 1)
        last = STEP * step + STEP if step + 1 == DISP // STEP else STEP * step + STEP - 2
        for d in range(max(STEP * step - 2, 0), last, 2):
            filtered(d)
            if d % STEP == STEP - 2:
                sent(d + 2 - STEP).start()
    for d in range(0, DISP, STEP):
        sent(d).wait()


def on_device(images, conv_weight, lift_weight, vol_weight):
    rows, cin, cols = images.shape
    outc, groups = vol_weight.shape[3:]
    feat = lift_weight.shape[0]
    per = feat // groups
    depth = (rows + 2) * groups
    padded = -(-3 * depth // 256) * 256
    m = 3 * rows * outc
    length = DISP * depth + padded
    vmem = pl.BlockSpec(memory_space=pltpu.VMEM)
    feats, vol_2 = pl.pallas_call(
        gather,
        out_shape=[
            jax.ShapeDtypeStruct((1 + STEP, per, depth, cols), f32),
            jax.ShapeDtypeStruct((2 * m, padded), bf16),
        ],
        in_specs=[pl.BlockSpec(memory_space=pltpu.HBM)] * 4,
        out_specs=[vmem] * 2,
        scratch_shapes=[
            pltpu.VMEM((2, rows + 4, cin, cols), f32),
            pltpu.VMEM((m, padded), f32),
            pltpu.VMEM((3 * cin, 9 * cin), bf16),
            pltpu.VMEM((feat, 3 * cin), bf16),
            pltpu.VMEM(conv_weight.shape, f32),
            pltpu.VMEM(lift_weight.shape, f32),
            pltpu.VMEM(vol_weight.shape, f32),
            pltpu.SemaphoreType.DMA((3 * CHUNKS + 2,)),
            pltpu.SemaphoreType.DMA((3 * CHUNKS + 2,)),
            pltpu.SemaphoreType.DMA((4,)),
            pltpu.SemaphoreType.REGULAR((3,)),
        ],
        compiler_params=pltpu.CompilerParams(
            vmem_limit_bytes=32 << 20, collective_id=0, has_side_effects=True
        ),
    )(*[pltpu.with_memory_space_constraint(a, pltpu.HBM) for a in (images, conv_weight, lift_weight, vol_weight)])
    flat = pl.pallas_call(
        compute,
        out_shape=jax.ShapeDtypeStruct((rows * outc, DISP, cols), f32),
        in_specs=[vmem] * 2,
        out_specs=pl.BlockSpec(memory_space=pltpu.HBM),
        scratch_shapes=[
            pltpu.VMEM((length, cols), bf16),
            pltpu.VMEM((length, cols), bf16),
            pltpu.VMEM((rows * outc, DISP, cols), f32),
            pltpu.SemaphoreType.DMA((DISP // STEP,)),
        ],
        compiler_params=pltpu.CompilerParams(
            vmem_limit_bytes=32 << 20
        ),
    )(feats, vol_2)
    return flat.reshape(rows, outc, DISP, cols)


def solution(mesh):
    placed = (P(("scenes", "rows"), None, None), P(), P(), P())
    return jax.shard_map(
        on_device,
        mesh=mesh,
        in_specs=placed,
        out_specs=P(("scenes", "rows"), None, None, None),
        check_vma=False,
    )
```

```python
import jax
import jax.numpy as jnp
from jax import lax
from jax.experimental import pallas as pl
from jax.experimental.pallas import tpu as pltpu
from jax.sharding import PartitionSpec as P

DISP = 48
CHUNK = 4
STEP = 8
WIDE = 4
CHUNKS = 4
MESH = pl.DeviceIdType.MESH
f32, bf16 = jnp.float32, jnp.bfloat16


def split(x):
    hi = x.astype(bf16)
    return hi, (x - hi.astype(f32)).astype(bf16)


def dot(a, b):
    return jnp.dot(a, b, preferred_element_type=f32)


def dot3(stacked, rows, hi, lo):
    both = dot(stacked, hi)
    return both[:rows] + both[rows:] + dot(stacked[:rows], lo)


def taps(y, size, lane):
    cols = y.shape[1]
    before = jnp.where(lane >= 1, pltpu.roll(y[:size], 1, 1), 0.0)
    after = jnp.where(lane < cols - 1, pltpu.roll(y[2 * size :], cols - 1, 1), 0.0)
    return y[size : 2 * size] + before + after


def turned(x, by, is_right):
    cols = x.shape[-1]
    cut = by % cols
    return x if cut == 0 else pltpu.roll(x, jnp.where(is_right, cols - cut, cut), 1)


def place_of():
    position = lax.axis_index("rows")
    quarter = lax.axis_size("rows") // 4
    starts = (position == quarter) | (position == 3 * quarter)
    ends = (position == quarter - 1) | (position == 3 * quarter - 1)
    is_right = (position < quarter) | (position >= 3 * quarter)
    return starts, ends, is_right


def stacked(x):
    hi, lo = split(x)
    return jnp.concatenate([hi, lo, hi], axis=0)


def weights(x):
    hi, lo = split(x)
    return jnp.concatenate([hi, hi, lo], axis=1)


def gather(
    images, cw_far, lw_far, vw_far, feats, vol_2,
    x, vol_f, conv_w, lift_w, cw, lw, vw, send, recv, load, ready,
):
    me, size = lax.axis_index("rows"), lax.axis_size("rows")
    starts, ends, is_right = place_of()
    half = size // 2
    rows, cin, cols = images.shape
    halo = rows + 2
    feat = lw.shape[0]
    outc, groups = vw.shape[3:]
    per = feat // groups
    depth = halo * groups
    lane = lax.broadcasted_iota(jnp.int32, (1, cols), 1)

    partner = lax.rem(me + half, size)
    late_up = (me == half - 1) | (me == size - 1)
    late_down = (me == 0) | (me == half)
    mated = late_up | late_down
    mate = jnp.where(me >= half, size + half - 1 - me, half - 1 - me)
    up = jnp.where(late_up, mate, lax.rem(me + 1, size))
    down = jnp.where(late_down, mate, lax.rem(me + size - 1, size))
    to_up, to_down = jnp.logical_not(ends), jnp.logical_not(starts)
    view_up = jnp.where(late_up, 1, 0)
    view_down = jnp.where(late_down, 1, 0)

    fills = [(cw_far, cw), (lw_far, lw), (vw_far, vw), (images, x.at[0, pl.ds(2, rows)])]
    fills = [pltpu.make_async_copy(a, b, load.at[n]) for n, (a, b) in enumerate(fills)]
    for one in fills:
        one.start()

    barrier = pltpu.get_barrier_semaphore()
    links = [(True, partner, 0), (to_up, up, 1), (to_down, down, 2)]

    def greet(other):
        pl.semaphore_signal(barrier, inc=1, device_id={"rows": other}, device_id_type=MESH)

    def confirm(other, n):
        pl.semaphore_signal(ready.at[n], inc=1, device_id={"rows": other}, device_id_type=MESH)

    def confirmed(n):
        pl.semaphore_wait(ready.at[n], 1)

    for there, other, _ in links:
        pl.when(there & (other > me))(lambda: greet(other))
    lower = sum(jnp.where(there & (other < me), 1, 0) for there, other, _ in links)
    pl.when(lower > 0)(lambda: pl.semaphore_wait(barrier, lower))
    for there, other, n in links:
        pl.when(there & (other < me))(lambda: confirm(other, (0, 2, 1)[n]))

    def copy(n, source, target, to):
        return pltpu.make_async_remote_copy(
            src_ref=source,
            dst_ref=target,
            send_sem=send.at[n],
            recv_sem=recv.at[n],
            device_id={"rows": to},
            device_id_type=MESH,
        )

    piece = cin // (CHUNKS // rows)
    places = [(r, pl.ds(a, piece)) for r in range(rows) for a in range(0, cin, piece)]
    above, here, below = pl.ds(0, 2), pl.ds(2, 2), pl.ds(rows + 2, 2)
    across = [copy(n, images.at[r, c], x.at[1, 2 + r, c], partner) for n, (r, c) in enumerate(places)]
    near_up = copy(CHUNKS, images.at[pl.ds(rows - 2, 2)], x.at[view_up, above], up)
    near_down = copy(CHUNKS + 1, images.at[pl.ds(0, 2)], x.at[view_down, below], down)
    relay_up = [
        copy(CHUNKS + 2 + n, x.at[1, 2 + r, c], x.at[1 - view_up, r, c], up)
        for n, (r, c) in enumerate(places)
    ]
    relay_down = [
        copy(2 * CHUNKS + 2 + n, x.at[1, 2 + r, c], x.at[1 - view_down, rows + 2 + r, c], down)
        for n, (r, c) in enumerate(places)
    ]
    held = (me >= size - size // 4) & jnp.logical_not(mated)

    def cross():
        for one in across:
            one.start()

    pl.when((partner < me) & jnp.logical_not(held))(cross)

    @pl.when(to_up)
    def _():
        pl.when(up > me)(lambda: confirmed(1))
        near_up.start()

    @pl.when(to_down)
    def _():
        pl.when(down > me)(lambda: confirmed(2))
        near_down.start()

    @pl.when(partner > me)
    def _():
        confirmed(0)
        cross()

    for one in fills:
        one.wait()

    conv_w[...] = weights(jnp.concatenate([cw[dr].reshape(3 * cin, cin) for dr in range(3)], axis=1))
    lift = jnp.concatenate([lw[pl.ds(k, groups, stride=per), :] for k in range(per)], axis=0)
    lift_w[...] = weights(lift)

    def features(v, h):
        parts = []
        for i in range(4):
            outside = (h == 0) & starts if i < 2 else (h == 1) & ends
            parts.append(split(jnp.where(outside, 0.0, x[v, 2 * h + i])))
        hi, lo = [
            jnp.concatenate(
                [jnp.concatenate([parts[t + k][i] for k in range(3)], axis=0) for t in range(2)], axis=1
            )
            for i in range(2)
        ]
        y = dot(conv_w[...], jnp.concatenate([hi, lo, hi], axis=0))
        hidden = []
        for n in range(2):
            z = jnp.maximum(taps(y[:, n * cols : (n + 1) * cols], cin, lane), 0.0)
            outside = (h == 0) & starts if n == 0 else (h == 1) & ends
            hidden.append(jnp.where(outside, 0.0, z))
        f = dot(lift_w[...], stacked(jnp.concatenate(hidden, axis=1)))
        top = pl.multiple_of(h * 2 * groups, 8)
        for n in range(2):
            for k in range(per):
                part = f[k * groups : (k + 1) * groups, n * cols : (n + 1) * cols]
                feats[1 - v, k, pl.ds(top + n * groups, groups), :] = part

    def spread(h):
        top = pl.multiple_of(h * 2 * groups, 8)
        for k in range(per):
            part = feats[1, k, pl.ds(top, 2 * groups), :]
            for b in range(1, STEP):
                feats[1 + b, k, pl.ds(top, 2 * groups), :] = turned(part, -b, is_right)

    vol_f[...] = jnp.zeros_like(vol_f)
    for dd in range(3):
        for dc in range(3):
            for r in range(rows):
                for dr in range(3):
                    top = (dc * rows + r) * outc
                    left = dd * depth + (r + dr) * groups
                    vol_f[top : top + outc, left : left + groups] = vw[dr, dd, dc] * (1.0 / per)
    m = 3 * rows * outc
    vol_2[:m], vol_2[m:] = split(vol_f[...])

    pl.when(held)(cross)
    odd = lax.rem(me, 2) == 1
    first = jnp.where(odd, 0, 1)

    def arrived(copies):
        for one in copies:
            one.wait_recv()

    pl.when(to_down & odd)(near_up.wait_recv)
    pl.when(to_up & jnp.logical_not(odd))(near_down.wait_recv)
    features(0, first)
    spread(first)

    for n in range(CHUNKS):
        across[n].wait_recv()
        pl.when(to_up)(relay_up[n].start)
        pl.when(to_down)(relay_down[n].start)

    pl.when(to_down & jnp.logical_not(odd))(near_up.wait_recv)
    pl.when(to_up & odd)(near_down.wait_recv)

    def rest(j, carry):
        v = jnp.where(mated, jnp.where(j == 2, 0, 1), jnp.where(j == 0, 0, 1))
        h = jnp.where(j == jnp.where(mated, 0, 1), first, 1 - first)
        due = j != jnp.where(mated, 1, 0)
        pl.when(due & to_down & (h == 0))(lambda: arrived(relay_up))
        pl.when(due & to_up & (h == 1))(lambda: arrived(relay_down))
        features(v, h)
        pl.when(v == 0)(lambda: spread(h))
        return carry

    lax.fori_loop(0, 3, rest, 0)

    for one in across:
        one.wait_send()

    pl.when(to_up)(near_up.wait_send)
    pl.when(to_down)(near_down.wait_send)

    @pl.when(to_up)
    def _():
        for one in relay_up:
            one.wait_send()

    @pl.when(to_down)
    def _():
        for one in relay_down:
            one.wait_send()


def compute(feats, vol_2, out, cost_hi, cost_lo, result, done):
    _, _, is_right = place_of()
    _, per, depth, cols = feats.shape
    m, padded = vol_2.shape
    m = m // 2
    lane = lax.broadcasted_iota(jnp.int32, (1, cols), 1)

    for buf in (cost_hi, cost_lo):
        buf[:depth] = jnp.zeros((depth, cols), bf16)
        tail = buf.shape[0] - (DISP + 1) * depth
        buf[(DISP + 1) * depth :] = jnp.zeros((tail, cols), bf16)
    reach = jnp.where(is_right, cols - 1 - lane, lane)

    def correlate(step):
        for base in range(0, depth, 16):
            at = slice(base, base + 16)
            right = [turned(feats[0, k, at, :], STEP * step, is_right) for k in range(per)]
            for b in range(STEP):
                d = STEP * step + b
                total = None
                for k in range(per):
                    term = feats[1 + b, k, at, :] * right[k]
                    total = term if total is None else total + term
                hi, lo = split(jnp.where(reach >= d, turned(total, b, is_right), 0.0))
                place = (d + 1) * depth + base
                cost_hi[place : place + 16, :] = hi
                cost_lo[place : place + 16, :] = lo

    def filtered(d):
        tops = [(d + n) * depth for n in range(WIDE)]
        hi, lo = [
            jnp.concatenate([buf[top : top + padded, :] for top in tops], axis=1)
            for buf in (cost_hi, cost_lo)
        ]
        y = dot3(vol_2[...], m, hi, lo)
        for h in range(WIDE):
            flat = result.reshape(m // 3 * DISP, cols)
            flat[pl.ds(d + h, m // 3, stride=DISP), :] = taps(y[:, h * cols : (h + 1) * cols], m // 3, lane)

    def sent(d):
        part = pl.ds(d, STEP)
        return pltpu.make_async_copy(result.at[:, part, :], out.at[:, part, :], done.at[d // STEP])

    made = 0
    correlate(0)
    for step in range(1, DISP // STEP + 1):
        if step < DISP // STEP:
            correlate(step)
        upto = DISP if step == DISP // STEP else (STEP * step - 2) // WIDE * WIDE
        for d in range(made, upto, WIDE):
            filtered(d)
            if (d + WIDE) % STEP == 0:
                sent(d + WIDE - STEP).start()
        made = upto

    for d in range(0, DISP, STEP):
        sent(d).wait()


def on_device(images, conv_weight, lift_weight, vol_weight):
    rows, cin, cols = images.shape
    outc, groups = vol_weight.shape[3:]
    feat = lift_weight.shape[0]
    per = feat // groups
    depth = (rows + 2) * groups
    padded = -(-3 * depth // 256) * 256
    m = 3 * rows * outc
    length = DISP * depth + padded
    vmem = pl.BlockSpec(memory_space=pltpu.VMEM)
    feats, vol_2 = pl.pallas_call(
        gather,
        out_shape=[
            jax.ShapeDtypeStruct((1 + STEP, per, depth, cols), f32),
            jax.ShapeDtypeStruct((2 * m, padded), bf16),
        ],
        in_specs=[pl.BlockSpec(memory_space=pltpu.HBM)] * 4,
        out_specs=[vmem] * 2,
        scratch_shapes=[
            pltpu.VMEM((2, rows + 4, cin, cols), f32),
            pltpu.VMEM((m, padded), f32),
            pltpu.VMEM((3 * cin, 9 * cin), bf16),
            pltpu.VMEM((feat, 3 * cin), bf16),
            pltpu.VMEM(conv_weight.shape, f32),
            pltpu.VMEM(lift_weight.shape, f32),
            pltpu.VMEM(vol_weight.shape, f32),
            pltpu.SemaphoreType.DMA((3 * CHUNKS + 2,)),
            pltpu.SemaphoreType.DMA((3 * CHUNKS + 2,)),
            pltpu.SemaphoreType.DMA((4,)),
            pltpu.SemaphoreType.REGULAR((3,)),
        ],
        compiler_params=pltpu.CompilerParams(
            vmem_limit_bytes=32 << 20, collective_id=0, has_side_effects=True,
        ),
    )(*[pltpu.with_memory_space_constraint(a, pltpu.HBM) for a in (images, conv_weight, lift_weight, vol_weight)])
    flat = pl.pallas_call(
        compute,
        out_shape=jax.ShapeDtypeStruct((rows * outc, DISP, cols), f32),
        in_specs=[vmem] * 2,
        out_specs=pl.BlockSpec(memory_space=pltpu.HBM),
        scratch_shapes=[
            pltpu.VMEM((length, cols), bf16),
            pltpu.VMEM((length, cols), bf16),
            pltpu.VMEM((rows * outc, DISP, cols), f32),
            pltpu.SemaphoreType.DMA((DISP // STEP,)),
        ],
        compiler_params=pltpu.CompilerParams(
            vmem_limit_bytes=32 << 20
        ),
    )(feats, vol_2)
    return flat.reshape(rows, outc, DISP, cols)


def solution(mesh):
    placed = (P(("scenes", "rows"), None, None), P(), P(), P())
    return jax.shard_map(
        on_device,
        mesh=mesh,
        in_specs=placed,
        out_specs=P(("scenes", "rows"), None, None, None),
        check_vma=False,
    )
```

```python
import jax
import jax.numpy as jnp
from jax import lax
from jax.experimental import pallas as pl
from jax.experimental.pallas import tpu as pltpu
from jax.sharding import PartitionSpec as P

DISP = 48
CHUNK = 4
STEP = 8
WIDE = 4
CHUNKS = 4
MESH = pl.DeviceIdType.MESH
f32, bf16 = jnp.float32, jnp.bfloat16


def split(x):
    hi = x.astype(bf16)
    return hi, (x - hi.astype(f32)).astype(bf16)


def dot(a, b):
    return jnp.dot(a, b, preferred_element_type=f32)


def dot3(stacked, rows, hi, lo):
    both = dot(stacked, hi)
    return both[:rows] + both[rows:] + dot(stacked[:rows], lo)


def taps(y, size, lane):
    cols = y.shape[1]
    before = jnp.where(lane >= 1, pltpu.roll(y[:size], 1, 1), 0.0)
    after = jnp.where(lane < cols - 1, pltpu.roll(y[2 * size :], cols - 1, 1), 0.0)
    return y[size : 2 * size] + before + after


def turned(x, by, is_right):
    cols = x.shape[-1]
    cut = by % cols
    return x if cut == 0 else pltpu.roll(x, jnp.where(is_right, cols - cut, cut), 1)


def place_of():
    position = lax.axis_index("rows")
    quarter = lax.axis_size("rows") // 4
    starts = (position == quarter) | (position == 3 * quarter)
    ends = (position == quarter - 1) | (position == 3 * quarter - 1)
    is_right = (position < quarter) | (position >= 3 * quarter)
    return starts, ends, is_right


def stacked(x):
    hi, lo = split(x)
    return jnp.concatenate([hi, lo, hi], axis=0)


def weights(x):
    hi, lo = split(x)
    return jnp.concatenate([hi, hi, lo], axis=1)


def gather(
    images, cw_far, lw_far, vw_far, feats, vol_2,
    x, vol_f, conv_w, lift_w, cw, lw, vw, send, recv, load, ready,
):
    me, size = lax.axis_index("rows"), lax.axis_size("rows")
    starts, ends, is_right = place_of()
    half = size // 2
    rows, cin, cols = images.shape
    halo = rows + 2
    feat = lw.shape[0]
    outc, groups = vw.shape[3:]
    per = feat // groups
    depth = halo * groups
    lane = lax.broadcasted_iota(jnp.int32, (1, cols), 1)

    partner = lax.rem(me + half, size)
    late_up = (me == half - 1) | (me == size - 1)
    late_down = (me == 0) | (me == half)
    mated = late_up | late_down
    mate = jnp.where(me >= half, size + half - 1 - me, half - 1 - me)
    up = jnp.where(late_up, mate, lax.rem(me + 1, size))
    down = jnp.where(late_down, mate, lax.rem(me + size - 1, size))
    to_up, to_down = jnp.logical_not(ends), jnp.logical_not(starts)
    view_up = jnp.where(late_up, 1, 0)
    view_down = jnp.where(late_down, 1, 0)

    fills = [(cw_far, cw), (lw_far, lw), (vw_far, vw), (images, x.at[0, pl.ds(2, rows)])]
    fills = [pltpu.make_async_copy(a, b, load.at[n]) for n, (a, b) in enumerate(fills)]
    for one in fills:
        one.start()

    barrier = pltpu.get_barrier_semaphore()
    links = [(True, partner, 0), (to_up, up, 1), (to_down, down, 2)]

    def greet(other):
        pl.semaphore_signal(barrier, inc=1, device_id={"rows": other}, device_id_type=MESH)

    def confirm(other, n):
        pl.semaphore_signal(ready.at[n], inc=1, device_id={"rows": other}, device_id_type=MESH)

    def confirmed(n):
        pl.semaphore_wait(ready.at[n], 1)

    for there, other, _ in links:
        pl.when(there & (other > me))(lambda: greet(other))
    lower = sum(jnp.where(there & (other < me), 1, 0) for there, other, _ in links)
    pl.when(lower > 0)(lambda: pl.semaphore_wait(barrier, lower))
    for there, other, n in links:
        pl.when(there & (other < me))(lambda: confirm(other, (0, 2, 1)[n]))

    def copy(n, source, target, to):
        return pltpu.make_async_remote_copy(
            src_ref=source,
            dst_ref=target,
            send_sem=send.at[n],
            recv_sem=recv.at[n],
            device_id={"rows": to},
            device_id_type=MESH,
        )

    piece = cin // (CHUNKS // rows)
    places = [(r, pl.ds(a, piece)) for r in range(rows) for a in range(0, cin, piece)]
    above, here, below = pl.ds(0, 2), pl.ds(2, 2), pl.ds(rows + 2, 2)
    across = [copy(n, images.at[r, c], x.at[1, 2 + r, c], partner) for n, (r, c) in enumerate(places)]
    near_up = copy(CHUNKS, images.at[pl.ds(rows - 2, 2)], x.at[view_up, above], up)
    near_down = copy(CHUNKS + 1, images.at[pl.ds(0, 2)], x.at[view_down, below], down)
    relay_up = [
        copy(CHUNKS + 2 + n, x.at[1, 2 + r, c], x.at[1 - view_up, r, c], up)
        for n, (r, c) in enumerate(places)
    ]
    relay_down = [
        copy(2 * CHUNKS + 2 + n, x.at[1, 2 + r, c], x.at[1 - view_down, rows + 2 + r, c], down)
        for n, (r, c) in enumerate(places)
    ]
    edge = starts | ends
    held = edge | (me >= size - size // 4) & jnp.logical_not(mated)

    def cross():
        for one in across:
            one.start()

    pl.when((partner < me) & jnp.logical_not(held))(cross)

    @pl.when(to_up)
    def _():
        pl.when(up > me)(lambda: confirmed(1))
        near_up.start()

    @pl.when(to_down)
    def _():
        pl.when(down > me)(lambda: confirmed(2))
        near_down.start()

    @pl.when((partner > me) & jnp.logical_not(held))
    def _():
        confirmed(0)
        cross()

    for one in fills:
        one.wait()

    conv_w[...] = weights(jnp.concatenate([cw[dr].reshape(3 * cin, cin) for dr in range(3)], axis=1))
    lift = jnp.concatenate([lw[pl.ds(k, groups, stride=per), :] for k in range(per)], axis=0)
    lift_w[...] = weights(lift)

    def features(v, h):
        parts = []
        for i in range(4):
            outside = (h == 0) & starts if i < 2 else (h == 1) & ends
            parts.append(split(jnp.where(outside, 0.0, x[v, 2 * h + i])))
        hi, lo = [
            jnp.concatenate(
                [jnp.concatenate([parts[t + k][i] for k in range(3)], axis=0) for t in range(2)], axis=1
            )
            for i in range(2)
        ]
        y = dot(conv_w[...], jnp.concatenate([hi, lo, hi], axis=0))
        hidden = []
        for n in range(2):
            z = jnp.maximum(taps(y[:, n * cols : (n + 1) * cols], cin, lane), 0.0)
            outside = (h == 0) & starts if n == 0 else (h == 1) & ends
            hidden.append(jnp.where(outside, 0.0, z))
        f = dot(lift_w[...], stacked(jnp.concatenate(hidden, axis=1)))
        top = pl.multiple_of(h * 2 * groups, 8)
        for n in range(2):
            for k in range(per):
                part = f[k * groups : (k + 1) * groups, n * cols : (n + 1) * cols]
                feats[1 - v, k, pl.ds(top + n * groups, groups), :] = part

    def spread(h):
        top = pl.multiple_of(h * 2 * groups, 8)
        for k in range(per):
            part = feats[1, k, pl.ds(top, 2 * groups), :]
            for b in range(1, STEP):
                feats[1 + b, k, pl.ds(top, 2 * groups), :] = turned(part, -b, is_right)

    vol_f[...] = jnp.zeros_like(vol_f)
    for dd in range(3):
        for dc in range(3):
            for r in range(rows):
                for dr in range(3):
                    top = (dc * rows + r) * outc
                    left = dd * depth + (r + dr) * groups
                    vol_f[top : top + outc, left : left + groups] = vw[dr, dd, dc] * (1.0 / per)
    m = 3 * rows * outc
    vol_2[:m], vol_2[m:] = split(vol_f[...])

    @pl.when(held)
    def _():
        pl.when(partner > me)(lambda: confirmed(0))
        cross()

    odd = lax.rem(me, 2) == 1
    first = jnp.where(odd, 0, 1)

    def arrived(copies):
        for one in copies:
            one.wait_recv()

    pl.when(to_down & odd)(near_up.wait_recv)
    pl.when(to_up & jnp.logical_not(odd))(near_down.wait_recv)
    features(0, first)
    spread(first)

    for n in range(CHUNKS):
        across[n].wait_recv()
        pl.when(to_up)(relay_up[n].start)
        pl.when(to_down)(relay_down[n].start)

    pl.when(to_down & jnp.logical_not(odd))(near_up.wait_recv)
    pl.when(to_up & odd)(near_down.wait_recv)

    def rest(j, carry):
        v = jnp.where(mated, jnp.where(j == 2, 0, 1), jnp.where(j == 0, 0, 1))
        h = jnp.where(j == jnp.where(mated, 0, 1), first, 1 - first)
        due = j != jnp.where(mated, 1, 0)
        pl.when(due & to_down & (h == 0))(lambda: arrived(relay_up))
        pl.when(due & to_up & (h == 1))(lambda: arrived(relay_down))
        features(v, h)
        pl.when(v == 0)(lambda: spread(h))
        return carry

    lax.fori_loop(0, 3, rest, 0)

    for one in across:
        one.wait_send()

    pl.when(to_up)(near_up.wait_send)
    pl.when(to_down)(near_down.wait_send)

    @pl.when(to_up)
    def _():
        for one in relay_up:
            one.wait_send()

    @pl.when(to_down)
    def _():
        for one in relay_down:
            one.wait_send()


def compute(feats, vol_2, out, cost_hi, cost_lo, result, done):
    _, _, is_right = place_of()
    _, per, depth, cols = feats.shape
    m, padded = vol_2.shape
    m = m // 2
    lane = lax.broadcasted_iota(jnp.int32, (1, cols), 1)

    for buf in (cost_hi, cost_lo):
        buf[:depth] = jnp.zeros((depth, cols), bf16)
        tail = buf.shape[0] - (DISP + 1) * depth
        buf[(DISP + 1) * depth :] = jnp.zeros((tail, cols), bf16)
    reach = jnp.where(is_right, cols - 1 - lane, lane)

    def correlate(step):
        for base in range(0, depth, 16):
            at = slice(base, base + 16)
            right = [turned(feats[0, k, at, :], STEP * step, is_right) for k in range(per)]
            for b in range(STEP):
                d = STEP * step + b
                total = None
                for k in range(per):
                    term = feats[1 + b, k, at, :] * right[k]
                    total = term if total is None else total + term
                hi, lo = split(jnp.where(reach >= d, turned(total, b, is_right), 0.0))
                place = (d + 1) * depth + base
                cost_hi[place : place + 16, :] = hi
                cost_lo[place : place + 16, :] = lo

    def filtered(d):
        tops = [(d + n) * depth for n in range(WIDE)]
        hi, lo = [
            jnp.concatenate([buf[top : top + padded, :] for top in tops], axis=1)
            for buf in (cost_hi, cost_lo)
        ]
        y = dot3(vol_2[...], m, hi, lo)
        for h in range(WIDE):
            flat = result.reshape(m // 3 * DISP, cols)
            flat[pl.ds(d + h, m // 3, stride=DISP), :] = taps(y[:, h * cols : (h + 1) * cols], m // 3, lane)

    def sent(d):
        part = pl.ds(d, STEP)
        return pltpu.make_async_copy(result.at[:, part, :], out.at[:, part, :], done.at[d // STEP])

    made = 0
    correlate(0)
    for step in range(1, DISP // STEP + 1):
        if step < DISP // STEP:
            correlate(step)
        upto = DISP if step == DISP // STEP else (STEP * step - 2) // WIDE * WIDE
        for d in range(made, upto, WIDE):
            filtered(d)
            if (d + WIDE) % STEP == 0:
                sent(d + WIDE - STEP).start()
        made = upto

    for d in range(0, DISP, STEP):
        sent(d).wait()


def on_device(images, conv_weight, lift_weight, vol_weight):
    rows, cin, cols = images.shape
    outc, groups = vol_weight.shape[3:]
    feat = lift_weight.shape[0]
    per = feat // groups
    depth = (rows + 2) * groups
    padded = -(-3 * depth // 256) * 256
    m = 3 * rows * outc
    length = DISP * depth + padded
    vmem = pl.BlockSpec(memory_space=pltpu.VMEM)
    feats, vol_2 = pl.pallas_call(
        gather,
        out_shape=[
            jax.ShapeDtypeStruct((1 + STEP, per, depth, cols), f32),
            jax.ShapeDtypeStruct((2 * m, padded), bf16),
        ],
        in_specs=[pl.BlockSpec(memory_space=pltpu.HBM)] * 4,
        out_specs=[vmem] * 2,
        scratch_shapes=[
            pltpu.VMEM((2, rows + 4, cin, cols), f32),
            pltpu.VMEM((m, padded), f32),
            pltpu.VMEM((3 * cin, 9 * cin), bf16),
            pltpu.VMEM((feat, 3 * cin), bf16),
            pltpu.VMEM(conv_weight.shape, f32),
            pltpu.VMEM(lift_weight.shape, f32),
            pltpu.VMEM(vol_weight.shape, f32),
            pltpu.SemaphoreType.DMA((3 * CHUNKS + 2,)),
            pltpu.SemaphoreType.DMA((3 * CHUNKS + 2,)),
            pltpu.SemaphoreType.DMA((4,)),
            pltpu.SemaphoreType.REGULAR((3,)),
        ],
        compiler_params=pltpu.CompilerParams(
            vmem_limit_bytes=32 << 20, collective_id=0, has_side_effects=True,
        ),
    )(*[pltpu.with_memory_space_constraint(a, pltpu.HBM) for a in (images, conv_weight, lift_weight, vol_weight)])
    flat = pl.pallas_call(
        compute,
        out_shape=jax.ShapeDtypeStruct((rows * outc, DISP, cols), f32),
        in_specs=[vmem] * 2,
        out_specs=pl.BlockSpec(memory_space=pltpu.HBM),
        scratch_shapes=[
            pltpu.VMEM((length, cols), bf16),
            pltpu.VMEM((length, cols), bf16),
            pltpu.VMEM((rows * outc, DISP, cols), f32),
            pltpu.SemaphoreType.DMA((DISP // STEP,)),
        ],
        compiler_params=pltpu.CompilerParams(
            vmem_limit_bytes=32 << 20
        ),
    )(feats, vol_2)
    return flat.reshape(rows, outc, DISP, cols)


def solution(mesh):
    placed = (P(("scenes", "rows"), None, None), P(), P(), P())
    return jax.shard_map(
        on_device,
        mesh=mesh,
        in_specs=placed,
        out_specs=P(("scenes", "rows"), None, None, None),
        check_vma=False,
    )
```

```python
import jax
import jax.numpy as jnp
from jax import lax
from jax.experimental import pallas as pl
from jax.experimental.pallas import tpu as pltpu
from jax.sharding import PartitionSpec as P

DISP = 48
CHUNK = 4
STEP = 8
WIDE = 4
CHUNKS = 4
MESH = pl.DeviceIdType.MESH
f32, bf16 = jnp.float32, jnp.bfloat16


def split(x):
    hi = x.astype(bf16)
    return hi, (x - hi.astype(f32)).astype(bf16)


def dot(a, b):
    return jnp.dot(a, b, preferred_element_type=f32)


def dot3(stacked, rows, hi, lo):
    both = dot(stacked, hi)
    return both[:rows] + both[rows:] + dot(stacked[:rows], lo)


def taps(y, size, lane):
    cols = y.shape[1]
    before = jnp.where(lane >= 1, pltpu.roll(y[:size], 1, 1), 0.0)
    after = jnp.where(lane < cols - 1, pltpu.roll(y[2 * size :], cols - 1, 1), 0.0)
    return y[size : 2 * size] + before + after


def turned(x, by, is_right):
    cols = x.shape[-1]
    cut = by % cols
    return x if cut == 0 else pltpu.roll(x, jnp.where(is_right, cols - cut, cut), 1)


def place_of():
    position = lax.axis_index("rows")
    quarter = lax.axis_size("rows") // 4
    starts = (position == quarter) | (position == 3 * quarter)
    ends = (position == quarter - 1) | (position == 3 * quarter - 1)
    is_right = (position < quarter) | (position >= 3 * quarter)
    return starts, ends, is_right


def stacked(x):
    hi, lo = split(x)
    return jnp.concatenate([hi, lo, hi], axis=0)


def weights(x):
    hi, lo = split(x)
    return jnp.concatenate([hi, hi, lo], axis=1)


def gather(
    images, cw_far, lw_far, vw_far, feats, vol_2,
    x, vol_f, conv_w, lift_w, cw, lw, vw, send, recv, load, ready,
):
    me, size = lax.axis_index("rows"), lax.axis_size("rows")
    starts, ends, is_right = place_of()
    half = size // 2
    rows, cin, cols = images.shape
    halo = rows + 2
    feat = lw.shape[0]
    outc, groups = vw.shape[3:]
    per = feat // groups
    depth = halo * groups
    lane = lax.broadcasted_iota(jnp.int32, (1, cols), 1)

    partner = lax.rem(me + half, size)
    late_up = (me == half - 1) | (me == size - 1)
    late_down = (me == 0) | (me == half)
    mated = late_up | late_down
    mate = jnp.where(me >= half, size + half - 1 - me, half - 1 - me)
    up = jnp.where(late_up, mate, lax.rem(me + 1, size))
    down = jnp.where(late_down, mate, lax.rem(me + size - 1, size))
    to_up, to_down = jnp.logical_not(ends), jnp.logical_not(starts)
    view_up = jnp.where(late_up, 1, 0)
    view_down = jnp.where(late_down, 1, 0)

    fills = [(cw_far, cw), (lw_far, lw), (vw_far, vw), (images, x.at[0, pl.ds(2, rows)])]
    fills = [pltpu.make_async_copy(a, b, load.at[n]) for n, (a, b) in enumerate(fills)]
    for one in fills:
        one.start()

    barrier = pltpu.get_barrier_semaphore()
    links = [(True, partner, 0), (to_up, up, 1), (to_down, down, 2)]

    def greet(other):
        pl.semaphore_signal(barrier, inc=1, device_id={"rows": other}, device_id_type=MESH)

    def confirm(other, n):
        pl.semaphore_signal(ready.at[n], inc=1, device_id={"rows": other}, device_id_type=MESH)

    def confirmed(n):
        pl.semaphore_wait(ready.at[n], 1)

    for there, other, _ in links:
        pl.when(there & (other > me))(lambda: greet(other))
    lower = sum(jnp.where(there & (other < me), 1, 0) for there, other, _ in links)
    pl.when(lower > 0)(lambda: pl.semaphore_wait(barrier, lower))
    for there, other, n in links:
        pl.when(there & (other < me))(lambda: confirm(other, (0, 2, 1)[n]))

    def copy(n, source, target, to):
        return pltpu.make_async_remote_copy(
            src_ref=source,
            dst_ref=target,
            send_sem=send.at[n],
            recv_sem=recv.at[n],
            device_id={"rows": to},
            device_id_type=MESH,
        )

    piece = cin // (CHUNKS // rows)
    places = [(r, pl.ds(a, piece)) for r in range(rows) for a in range(0, cin, piece)]
    above, here, below = pl.ds(0, 2), pl.ds(2, 2), pl.ds(rows + 2, 2)
    across = [copy(n, images.at[r, c], x.at[1, 2 + r, c], partner) for n, (r, c) in enumerate(places)]
    near_up = copy(CHUNKS, images.at[pl.ds(rows - 2, 2)], x.at[view_up, above], up)
    near_down = copy(CHUNKS + 1, images.at[pl.ds(0, 2)], x.at[view_down, below], down)
    relay_up = [
        copy(CHUNKS + 2 + n, x.at[1, 2 + r, c], x.at[1 - view_up, r, c], up)
        for n, (r, c) in enumerate(places)
    ]
    relay_down = [
        copy(2 * CHUNKS + 2 + n, x.at[1, 2 + r, c], x.at[1 - view_down, rows + 2 + r, c], down)
        for n, (r, c) in enumerate(places)
    ]
    edge = starts | ends
    held = edge | (me >= size - size // 4) & jnp.logical_not(mated)

    def cross():
        for one in across:
            one.start()

    pl.when((partner < me) & jnp.logical_not(held))(cross)

    @pl.when(to_up)
    def _():
        pl.when(up > me)(lambda: confirmed(1))
        near_up.start()

    @pl.when(to_down)
    def _():
        pl.when(down > me)(lambda: confirmed(2))
        near_down.start()

    @pl.when((partner > me) & jnp.logical_not(held))
    def _():
        confirmed(0)
        cross()

    for one in fills:
        one.wait()

    conv_w[...] = weights(jnp.concatenate([cw[dr].reshape(3 * cin, cin) for dr in range(3)], axis=1))
    lift = jnp.concatenate([lw[pl.ds(k, groups, stride=per), :] for k in range(per)], axis=0)
    lift_w[...] = weights(lift)

    def features(v, h):
        parts = []
        for i in range(4):
            outside = (h == 0) & starts if i < 2 else (h == 1) & ends
            parts.append(split(jnp.where(outside, 0.0, x[v, 2 * h + i])))
        hi, lo = [
            jnp.concatenate(
                [jnp.concatenate([parts[t + k][i] for k in range(3)], axis=0) for t in range(2)], axis=1
            )
            for i in range(2)
        ]
        y = dot(conv_w[...], jnp.concatenate([hi, lo, hi], axis=0))
        hidden = []
        for n in range(2):
            z = jnp.maximum(taps(y[:, n * cols : (n + 1) * cols], cin, lane), 0.0)
            outside = (h == 0) & starts if n == 0 else (h == 1) & ends
            hidden.append(jnp.where(outside, 0.0, z))
        f = dot(lift_w[...], stacked(jnp.concatenate(hidden, axis=1)))
        top = pl.multiple_of(h * 2 * groups, 8)
        for n in range(2):
            for k in range(per):
                part = f[k * groups : (k + 1) * groups, n * cols : (n + 1) * cols]
                feats[1 - v, k, pl.ds(top + n * groups, groups), :] = part

    def spread(h):
        top = pl.multiple_of(h * 2 * groups, 8)
        for k in range(per):
            part = feats[1, k, pl.ds(top, 2 * groups), :]
            for b in range(1, STEP):
                feats[1 + b, k, pl.ds(top, 2 * groups), :] = turned(part, -b, is_right)

    vol_f[...] = jnp.zeros_like(vol_f)
    for dd in range(3):
        for dc in range(3):
            for r in range(rows):
                for dr in range(3):
                    top = (dc * rows + r) * outc
                    left = dd * depth + (r + dr) * groups
                    vol_f[top : top + outc, left : left + groups] = vw[dr, dd, dc] * (1.0 / per)
    m = 3 * rows * outc
    vol_2[:m], vol_2[m:] = split(vol_f[...])

    @pl.when(held)
    def _():
        pl.when(partner > me)(lambda: confirmed(0))
        cross()

    odd = lax.rem(me, 2) == 1
    first = jnp.where(odd, 0, 1)

    def arrived(copies):
        for one in copies:
            one.wait_recv()

    pl.when(to_down & odd)(near_up.wait_recv)
    pl.when(to_up & jnp.logical_not(odd))(near_down.wait_recv)
    features(0, first)
    spread(first)

    for n in range(CHUNKS):
        across[n].wait_recv()
        pl.when(to_up)(relay_up[n].start)
        pl.when(to_down)(relay_down[n].start)

    pl.when(to_down & jnp.logical_not(odd))(near_up.wait_recv)
    pl.when(to_up & odd)(near_down.wait_recv)

    def rest(j, carry):
        v = jnp.where(mated, jnp.where(j == 2, 0, 1), jnp.where(j == 0, 0, 1))
        h = jnp.where(j == jnp.where(mated, 0, 1), first, 1 - first)
        due = j != jnp.where(mated, 1, 0)
        pl.when(due & to_down & (h == 0))(lambda: arrived(relay_up))
        pl.when(due & to_up & (h == 1))(lambda: arrived(relay_down))
        features(v, h)
        pl.when(v == 0)(lambda: spread(h))
        return carry

    lax.fori_loop(0, 3, rest, 0)

    for one in across:
        one.wait_send()

    pl.when(to_up)(near_up.wait_send)
    pl.when(to_down)(near_down.wait_send)

    @pl.when(to_up)
    def _():
        for one in relay_up:
            one.wait_send()

    @pl.when(to_down)
    def _():
        for one in relay_down:
            one.wait_send()


def compute(feats, vol_2, out, cost_hi, cost_lo, result, done):
    _, _, is_right = place_of()
    _, per, depth, cols = feats.shape
    m, padded = vol_2.shape
    m = m // 2
    lane = lax.broadcasted_iota(jnp.int32, (1, cols), 1)

    for buf in (cost_hi, cost_lo):
        buf[:depth] = jnp.zeros((depth, cols), bf16)
        tail = buf.shape[0] - (DISP + 1) * depth
        buf[(DISP + 1) * depth :] = jnp.zeros((tail, cols), bf16)
    reach = jnp.where(is_right, cols - 1 - lane, lane)

    def correlate(step):
        for base in range(0, depth, 16):
            at = slice(base, base + 16)
            right = [turned(feats[0, k, at, :], STEP * step, is_right) for k in range(per)]
            for b in range(STEP):
                d = STEP * step + b
                total = None
                for k in range(per):
                    term = feats[1 + b, k, at, :] * right[k]
                    total = term if total is None else total + term
                hi, lo = split(jnp.where(reach >= d, turned(total, b, is_right), 0.0))
                place = (d + 1) * depth + base
                cost_hi[place : place + 16, :] = hi
                cost_lo[place : place + 16, :] = lo

    def filtered(d):
        tops = [(d + n) * depth for n in range(WIDE)]
        hi, lo = [
            jnp.concatenate([buf[top : top + padded, :] for top in tops], axis=1)
            for buf in (cost_hi, cost_lo)
        ]
        y = dot3(vol_2[...], m, hi, lo)
        for h in range(WIDE):
            flat = result.reshape(m // 3 * DISP, cols)
            flat[pl.ds(d + h, m // 3, stride=DISP), :] = taps(y[:, h * cols : (h + 1) * cols], m // 3, lane)

    def sent(d):
        part = pl.ds(d, WIDE)
        return pltpu.make_async_copy(result.at[:, part, :], out.at[:, part, :], done.at[d // WIDE])

    made = 0
    correlate(0)
    for step in range(1, DISP // STEP + 1):
        if step < DISP // STEP:
            correlate(step)
        upto = DISP if step == DISP // STEP else (STEP * step - 2) // WIDE * WIDE
        for d in range(made, upto, WIDE):
            filtered(d)
            sent(d).start()
        made = upto

    for d in range(0, DISP, WIDE):
        sent(d).wait()


def on_device(images, conv_weight, lift_weight, vol_weight):
    rows, cin, cols = images.shape
    outc, groups = vol_weight.shape[3:]
    feat = lift_weight.shape[0]
    per = feat // groups
    depth = (rows + 2) * groups
    padded = -(-3 * depth // 256) * 256
    m = 3 * rows * outc
    length = DISP * depth + padded
    vmem = pl.BlockSpec(memory_space=pltpu.VMEM)
    feats, vol_2 = pl.pallas_call(
        gather,
        out_shape=[
            jax.ShapeDtypeStruct((1 + STEP, per, depth, cols), f32),
            jax.ShapeDtypeStruct((2 * m, padded), bf16),
        ],
        in_specs=[pl.BlockSpec(memory_space=pltpu.HBM)] * 4,
        out_specs=[vmem] * 2,
        scratch_shapes=[
            pltpu.VMEM((2, rows + 4, cin, cols), f32),
            pltpu.VMEM((m, padded), f32),
            pltpu.VMEM((3 * cin, 9 * cin), bf16),
            pltpu.VMEM((feat, 3 * cin), bf16),
            pltpu.VMEM(conv_weight.shape, f32),
            pltpu.VMEM(lift_weight.shape, f32),
            pltpu.VMEM(vol_weight.shape, f32),
            pltpu.SemaphoreType.DMA((3 * CHUNKS + 2,)),
            pltpu.SemaphoreType.DMA((3 * CHUNKS + 2,)),
            pltpu.SemaphoreType.DMA((4,)),
            pltpu.SemaphoreType.REGULAR((3,)),
        ],
        compiler_params=pltpu.CompilerParams(
            vmem_limit_bytes=32 << 20, collective_id=0, has_side_effects=True,
        ),
    )(*[pltpu.with_memory_space_constraint(a, pltpu.HBM) for a in (images, conv_weight, lift_weight, vol_weight)])
    flat = pl.pallas_call(
        compute,
        out_shape=jax.ShapeDtypeStruct((rows * outc, DISP, cols), f32),
        in_specs=[vmem] * 2,
        out_specs=pl.BlockSpec(memory_space=pltpu.HBM),
        scratch_shapes=[
            pltpu.VMEM((length, cols), bf16),
            pltpu.VMEM((length, cols), bf16),
            pltpu.VMEM((rows * outc, DISP, cols), f32),
            pltpu.SemaphoreType.DMA((DISP // WIDE,)),
        ],
        compiler_params=pltpu.CompilerParams(
            vmem_limit_bytes=32 << 20
        ),
    )(feats, vol_2)
    return flat.reshape(rows, outc, DISP, cols)


def solution(mesh):
    placed = (P(("scenes", "rows"), None, None), P(), P(), P())
    return jax.shard_map(
        on_device,
        mesh=mesh,
        in_specs=placed,
        out_specs=P(("scenes", "rows"), None, None, None),
        check_vma=False,
    )
```
